256 devices in a mesh: row: 64 (over x, z, core), col: 4 (over y).
Axes of the slice: x: 4, y: 4, z: 8, core: 2. Of those that a mesh axis runs over, the one named last changes fastest.
Arguments:
- pivot_block: float32 [512, 512], P('row', 'col'), as said below
- pivot_tangent: float32 [512, 512], P('row', 'col'), as said below
- panel_block: float32 [65536, 512], P('row', 'col'), may hold values from -1.5 to 1.5
- panel_tangent: float32 [65536, 512], P('row', 'col'), may hold values from -1.5 to 1.5
- strip_block: float32 [65536, 2048], P('row', 'col'), may hold values from -6 to 6
- strip_tangent: float32 [65536, 2048], P('row', 'col'), may hold values from -6 to 6
Outputs:
- pivot_factor: float32 [512, 512], P('row', 'col')
- pivot_factor_tangent: float32 [512, 512], P('row', 'col')
- panel_factor: float32 [65536, 512], P('row', 'col')
- panel_factor_tangent: float32 [65536, 512], P('row', 'col')
- strip_updated: float32 [65536, 2048], P('row', 'col')
- strip_updated_tangent: float32 [65536, 2048], P('row', 'col')
The draws below stay inside these ranges and needn't reach their ends.
Inputs may be any that keep to these rules, and one draw needn't show every extreme that they name: `pivot_block`: symmetric positive definite; its smallest eigenvalue is at least 0.05. `pivot_tangent`: symmetric.
All inputs are finite; a program needn't handle non-finite values.
Results may differ from the reference program's by a relative error of at most 0.0003.
Values sent between devices are 32-bit elements; how exact they have to be, the bound alone decides.
No kernel may reach another device: no remote copies, remote signals or barrier semaphores. Data moves between devices by JAX's collectives and lax.ppermute only.
A program may use at most 128 MiB of HBM per device.

```python
import math
import jax
import jax.numpy as jnp
from jax import lax

PIVOT = 512
ROWS_DEV = 1024
TILE = 8
ROWS = 65536
STRIP = 2048
N_ROW = 64
N_COL = 4


def scaled_distance(key, length):
    places = jax.random.uniform(jax.random.fold_in(key, 5), (PIVOT, 2), jnp.float32, 0.0, 1.0)
    across = places[:, None, 0] - places[None, :, 0]
    along = places[:, None, 1] - places[None, :, 1]
    distance = jnp.sqrt(across * across + along * along)
    return math.sqrt(3.0) * distance / length


def draw_pivot_block(key, part):
    length_key = jax.random.fold_in(key, 7)
    nugget_key = jax.random.fold_in(key, 13)
    length = jax.random.uniform(length_key, (), jnp.float32, 0.12, 0.2)
    nugget = jax.random.uniform(nugget_key, (PIVOT,), jnp.float32, 0.08, 0.2)
    scaled = scaled_distance(key, length)
    kernel = (1.0 + scaled) * jnp.exp(-scaled)
    return kernel + jnp.diag(nugget)


def draw_pivot_tangent(key, part):
    length_key = jax.random.fold_in(key, 7)
    noise_key = jax.random.fold_in(key, 23)
    length = jax.random.uniform(length_key, (), jnp.float32, 0.12, 0.2)
    raw_values = jnp.clip(jax.random.normal(noise_key, (PIVOT, PIVOT), jnp.float32), -4.0, 4.0)
    scaled = scaled_distance(key, length)
    smooth_part = 0.5 * scaled * scaled * jnp.exp(-scaled)
    return smooth_part + (raw_values + raw_values.T) * (0.25 / math.sqrt(PIVOT))


def block_scale(rng, shape, split, low, largest):
    gain, own = 1.0, jax.random.fold_in(rng, 6)
    for axis_at, blocks in split:
        steps = jnp.exp(jax.random.uniform(jax.random.fold_in(own, axis_at), (blocks,), jnp.float32, low / len(split), largest / len(split)))
        gain = gain * jnp.repeat(steps, shape[axis_at] // blocks).reshape([-1 if axis == axis_at else 1 for axis in range(len(shape))])
    return gain


def bell_draw(own_key, extent, deviation, most, split=(), kind=jnp.bfloat16):
    factor_of = block_scale(own_key, extent, split, -0.22, 0.18) if split else 1.0
    entries = jax.random.normal(own_key, extent, jnp.float32) * deviation * factor_of
    return jnp.minimum(jnp.maximum(entries, -most), most).astype(kind)


def setup_inputs(seed: int = 0) -> dict:
    seeds = jax.random.split(jax.random.key(seed), 7)
    return {
        "pivot_block": draw_pivot_block(jax.random.fold_in(seeds[6], 71), 0),
        "pivot_tangent": draw_pivot_tangent(jax.random.fold_in(seeds[6], 71), 0),
        "panel_block": bell_draw(seeds[2], (ROWS, PIVOT), 0.25, 1.5, ((0, 64), (1, 4)), jnp.float32),
        "panel_tangent": bell_draw(seeds[3], (ROWS, PIVOT), 0.25, 1.5, ((0, 64), (1, 4)), jnp.float32),
        "strip_block": bell_draw(seeds[4], (ROWS, STRIP), 1.0, 6.0, ((0, 64), (1, 4)), jnp.float32),
        "strip_tangent": bell_draw(seeds[5], (ROWS, STRIP), 1.0, 6.0, ((0, 64), (1, 4)), jnp.float32),
    }


def strip_order(matrix):
    blocks = matrix.reshape(N_ROW, ROWS_DEV, PIVOT)[:, :N_COL * TILE]
    return blocks.reshape(N_ROW, N_COL, TILE, PIVOT).transpose(1, 0, 2, 3).reshape(N_COL * N_ROW * TILE, PIVOT)

def reference(pivot_block, pivot_tangent, panel_block, panel_tangent, strip_block, strip_tangent):
    highest = lax.Precision.HIGHEST
    pivot_factor = jnp.linalg.cholesky(pivot_block)
    identity = jnp.eye(PIVOT, dtype=pivot_block.dtype)
    inverse = lax.linalg.triangular_solve(pivot_factor, identity, left_side=True, lower=True)
    mixed = jnp.dot(jnp.dot(inverse, pivot_tangent, precision=highest), inverse.T, precision=highest)
    halved = jnp.tril(mixed, -1) + 0.5 * jnp.diag(jnp.diag(mixed))
    pivot_change = jnp.dot(pivot_factor, halved, precision=highest)
    panel_factor = jnp.dot(panel_block, inverse.T, precision=highest)
    panel_change = jnp.dot(panel_tangent - jnp.dot(panel_factor, pivot_change.T, precision=highest), inverse.T, precision=highest)
    strip_rows = strip_order(panel_factor)
    strip_rows_tangent = strip_order(panel_change)
    strip_updated = strip_block - jnp.dot(panel_factor, strip_rows.T, precision=highest)
    strip_changed = strip_tangent - jnp.dot(panel_change, strip_rows.T, precision=highest) - jnp.dot(panel_factor, strip_rows_tangent.T, precision=highest)
    return (pivot_factor, pivot_change, panel_factor, panel_change, strip_updated, strip_changed)
```

```python
import jax
import jax.numpy as jnp
from jax import lax
from jax.experimental import pallas as pl
from jax.experimental.pallas import tpu as pltpu
from jax.sharding import PartitionSpec as P

PIVOT = 512
HALF = PIVOT // 2
BLOCK = 64
PANEL_TILE = 256
F32 = jnp.float32
BF16 = jnp.bfloat16
N_X, N_Z, N_CORE, N_Y = 4, 8, 2, 4


def exact_nt(a, b):
    return lax.dot_general(
        a, b, (((1,), (1,)), ((), ())), precision=lax.Precision.HIGHEST, preferred_element_type=F32
    )


def exact_nn(a, b):
    return lax.dot_general(
        a, b, (((1,), (0,)), ((), ())), precision=lax.Precision.HIGHEST, preferred_element_type=F32
    )


def halves(x):
    high = x.astype(BF16)
    return high, (x - high.astype(F32)).astype(BF16)


def nt(a, b):
    return lax.dot_general(a, b, (((1,), (1,)), ((), ())), preferred_element_type=F32)


def split_nt(a, b):
    return nt(a[0], b[0]) + (nt(a[0], b[1]) + nt(a[1], b[0]))


def lane(x, k):
    return jnp.broadcast_to(x[:, k : k + 1], (8, 128))


def sub(x, k):
    return jnp.broadcast_to(x[k : k + 1, :], (8, 128))


def factor_block(rows):
    rows = list(rows)
    sublane = lax.broadcasted_iota(jnp.int32, (8, 128), 0)
    done = []
    for s in range(8):
        cols = {b: [lane(rows[b], 8 * s + k) for k in range(8)] for b in range(s, 8)}
        corner = [[sub(cols[s][k], i) if i >= k else None for k in range(8)] for i in range(8)]
        scale = None
        for k in range(8):
            r = 1.0 / corner[k][k]
            m = [corner[i][k] * r if i > k else None for i in range(8)]
            for i in range(k + 1, 8):
                for j in range(k + 1, i + 1):
                    corner[i][j] = corner[i][j] - m[i] * corner[j][k]
            pivot_row = sub(rows[s], k)
            for b in range(s, 8):
                mul = cols[b][k] * r
                if b == s:
                    mul = jnp.where(sublane > k, mul, 0.0)
                for j in range(k + 1, 8):
                    cols[b][j] = cols[b][j] - mul * corner[j][k]
                rows[b] = rows[b] - mul * pivot_row
            y = lax.rsqrt(corner[k][k])
            y = y * (1.5 - 0.5 * corner[k][k] * y * y)
            scale = y if scale is None else jnp.where(sublane == k, y, scale)
        done.append(rows[s] * scale)
    return done


def merge(l_ref, x_ref, lo, h):
    a, b, c = lo, lo + h, lo + 2 * h
    t = exact_nn(l_ref[b:c, a:b], x_ref[a:b, a:b])
    x_ref[b:c, a:b] = -exact_nn(x_ref[b:c, b:c], t)


def forward(w_ref, l_ref, x_ref, lo, h):
    a, b, c = lo, lo + h, lo + 2 * h
    l21 = exact_nt(w_ref[b:c, a:b], x_ref[a:b, a:b])
    l_ref[b:c, a:b] = l21
    w_ref[b:c, b:c] = w_ref[b:c, b:c] - exact_nt(l21, l21)


def after_block(w_ref, l_ref, x_ref, j):
    h = BLOCK
    while h < HALF:
        if j % 2 == 1:
            merge(l_ref, x_ref, (j - 1) * h, h)
            j //= 2
            h *= 2
        else:
            forward(w_ref, l_ref, x_ref, j * h, h)
            return


def factor_blocks(w_ref, l_ref, x_ref, first, last):
    ri = lax.broadcasted_iota(jnp.int32, (BLOCK, BLOCK), 0)
    ci = lax.broadcasted_iota(jnp.int32, (BLOCK, BLOCK), 1)
    wide = lax.broadcasted_iota(jnp.int32, (BLOCK, 128), 1)
    eye = jnp.where(ri == ci, 1.0, 0.0).astype(F32)
    zero = jnp.zeros((BLOCK, BLOCK), F32)

    def step(j, carry):
        rows = pl.ds(pl.multiple_of(j * BLOCK, BLOCK), BLOCK)
        lanes = pl.ds(pl.multiple_of((j // 2) * 128, 128), 128)
        full = w_ref[rows, lanes]
        d = jnp.where(j % 2 == 0, full[:, :BLOCK], full[:, BLOCK:])
        both = jnp.concatenate([d, eye], axis=1)
        both = factor_block([both[8 * b : 8 * b + 8] for b in range(8)])
        both = jnp.concatenate(both, axis=0)
        low = jnp.where(ri >= ci, both[:, :BLOCK].T, 0.0)
        inverse = jnp.where(ri >= ci, both[:, BLOCK:], 0.0)
        for side in range(2):

            @pl.when(j % 2 == side)
            def _():
                put = lambda v: jnp.concatenate([v, zero] if side == 0 else [zero, v], 1)
                x_ref[rows, lanes] = put(inverse)
                l_ref[rows, lanes] = jnp.where(wide >= side * BLOCK, put(low), l_ref[rows, lanes])

        for jj in range(first, last):

            @pl.when(j == jj)
            def _():
                after_block(w_ref, l_ref, x_ref, jj)

        return carry

    lax.fori_loop(first, last, step, 0)


def places(at_ref):
    x, z, core = at_ref[2], at_ref[3], at_ref[4]
    for s_core in range(N_CORE):
        for s_x in range(N_X):
            for s_z in range(N_Z):
                row = (lax.rem(x + N_X - s_x, N_X) * N_Z + lax.rem(z + N_Z - s_z, N_Z)) * N_CORE
                yield s_core, s_x, s_z, row + lax.rem(core + N_CORE - s_core, N_CORE)


def spread(at_ref, pieces, tile, out_ref):
    col = at_ref[1]
    lanes = [pl.ds(pl.multiple_of(lax.rem(col + N_Y - s, N_Y) * 128, 128), 128) for s in range(N_Y)]
    for s_core, s_x, s_z, row in places(at_ref):
        piece = pieces[s_core * N_X + s_x]
        rows = pl.ds(pl.multiple_of(row * 8, 8), 8)
        for s_y in range(N_Y):
            out_ref[rows, lanes[s_y]] = piece[s_z, s_y, tile]


def first_half(*refs):
    at_ref, pieces = refs[0], refs[1:9]
    w_out, l_ref, x_ref, w_ref = refs[9:]
    spread(at_ref, pieces, 0, w_ref)
    l_ref[...] = jnp.zeros((PIVOT, HALF), F32)
    x_ref[...] = jnp.zeros((HALF, HALF), F32)
    factor_blocks(w_ref, l_ref, x_ref, 0, HALF // BLOCK)
    a = slice(0, HALF)
    b = slice(HALF, PIVOT)
    l21 = exact_nt(w_ref[b, a], x_ref[...])
    l_ref[b, :] = l21
    w_out[...] = w_ref[b, b] - exact_nt(l21, l21)


def second_half(w_in, l_in, x_in, l_ref, x_ref, w_ref, l22, x22):
    a = slice(0, HALF)
    b = slice(HALF, PIVOT)
    w_ref[...] = w_in[...]
    l22[...] = jnp.zeros((HALF, HALF), F32)
    x22[...] = jnp.zeros((HALF, HALF), F32)
    factor_blocks(w_ref, l22, x22, 0, HALF // BLOCK)
    l_ref[:, a] = l_in[...]
    l_ref[a, b] = jnp.zeros((HALF, HALF), F32)
    l_ref[b, b] = l22[...]
    x_ref[a, a] = x_in[...]
    x_ref[a, b] = jnp.zeros((HALF, HALF), F32)
    x_ref[b, b] = x22[...]
    x_ref[b, a] = -exact_nn(x22[...], exact_nn(l_in[b, :], x_in[...]))


def upper_nt(a, b):
    left = split_nt([v[:, :HALF] for v in a], [v[:HALF, :HALF] for v in b])
    right = split_nt(a, [v[HALF:, :] for v in b])
    return jnp.concatenate([left, right], axis=1)


def tangent_factor(x_ref, ad_ref, phi_ref):
    h = HALF
    x11, x21, x22 = x_ref[:h, :h], x_ref[h:, :h], x_ref[h:, h:]
    t11 = exact_nn(x11, ad_ref[:h, :h])
    t21 = exact_nn(x21, ad_ref[:h, :h]) + exact_nn(x22, ad_ref[h:, :h])
    t22 = exact_nn(x21, ad_ref[:h, h:]) + exact_nn(x22, ad_ref[h:, h:])
    ri = lax.broadcasted_iota(jnp.int32, (h, h), 0)
    ci = lax.broadcasted_iota(jnp.int32, (h, h), 1)
    weight = jnp.where(ri > ci, 1.0, jnp.where(ri == ci, 0.5, 0.0)).astype(F32)
    phi_ref[:h, :h] = exact_nt(t11, x11) * weight
    phi_ref[h:, :h] = exact_nt(t21, x11)
    phi_ref[h:, h:] = (exact_nt(t21, x21) + exact_nt(t22, x22)) * weight
    phi_ref[:h, h:] = jnp.zeros((h, h), F32)


def panel(*refs):
    at_ref, l_ref, x_ref = refs[:3]
    pieces = refs[3:11]
    parts, tangent_parts = refs[11:15], refs[15:19]
    strip_ref, strip_tangent_ref = refs[19:21]
    factor_out, change_out, panel_out, panel_change_out, strip_out, strip_change_out = refs[21:27]
    ad, raw, phi, xs, phis, qs, qds, rows_ref, done_ref = refs[27:]
    col = at_ref[1]
    whole = slice(None)

    @pl.when(pl.program_id(0) == 0)
    def _():
        spread(at_ref, pieces, 0, ad)
        spread(at_ref, pieces, 1, raw.at[0])
        spread(at_ref, pieces, 2, raw.at[1])
        tangent_factor(x_ref, ad, phi)
        own = pl.ds(pl.multiple_of(at_ref[0] * 8, 8), 8)
        lanes = pl.ds(pl.multiple_of(col * 128, 128), 128)
        factor_out[...] = l_ref[own, lanes]
        change_out[...] = exact_nn(l_ref[own, :], phi[:, lanes])
        xs[0], xs[1] = halves(x_ref[...])
        phis[0], phis[1] = halves(phi[...])
        solved = upper_nt(halves(raw[...].reshape(2 * PIVOT, PIVOT)), [xs[0], xs[1]])
        q = halves(solved[:PIVOT])
        qs[0], qs[1] = q
        qds[0], qds[1] = halves(solved[PIVOT:] - upper_nt(q, [phis[0], phis[1]]))

    for shift, part, tangent_part in zip((0, 3, 1, 2), parts, tangent_parts):
        lanes = pl.ds(pl.multiple_of(lax.rem(col + shift, N_Y) * 128, 128), 128)
        for at, value in ((0, part[...]), (PANEL_TILE, tangent_part[...])):
            high, low = halves(value)
            rows_ref[0, at : at + PANEL_TILE, lanes] = high
            rows_ref[1, at : at + PANEL_TILE, lanes] = low
    solved = upper_nt([rows_ref[0], rows_ref[1]], [xs[0], xs[1]])
    factor = solved[:PANEL_TILE]
    factor_halves = halves(factor)
    change = solved[PANEL_TILE:] - upper_nt(factor_halves, [phis[0], phis[1]])
    change_halves = halves(change)
    done_ref[0] = factor
    done_ref[1] = change
    lanes = pl.ds(pl.multiple_of(col * 128, 128), 128)
    panel_out[...] = done_ref[0, :, lanes]
    panel_change_out[...] = done_ref[1, :, lanes]
    q = [qs[0], qs[1]]
    strip_out[...] = strip_ref[...] - split_nt(factor_halves, q)
    strip_change_out[...] = strip_tangent_ref[...] - (
        split_nt(change_halves, q) + split_nt(factor_halves, [qds[0], qds[1]])
    )


def row_shift(d_x, d_z, d_core):
    def to(r):
        core, z, x = r % N_CORE, (r // N_CORE) % N_Z, r // (N_CORE * N_Z)
        return (((x + d_x) % N_X) * N_Z + (z + d_z) % N_Z) * N_CORE + (core + d_core) % N_CORE

    return [(r, to(r)) for r in range(N_X * N_Z * N_CORE)]


def along_y(x, s):
    return lax.ppermute(x, "col", [(c, (c + s) % N_Y) for c in range(N_Y)])


def along_row(x, *shift):
    return lax.ppermute(x, "row", row_shift(*shift))


def gather_pieces(by_y):
    held = jnp.stack(by_y)
    held = jnp.stack([held] + [along_row(held, 0, s, 0) for s in range(1, N_Z)])
    by_x = [held] + [along_row(held, s, 0, 0) for s in range(1, N_X)]
    return by_x + [along_row(v, 0, 0, 1) for v in by_x]


def body(pivot_block, pivot_tangent, panel_block, panel_tangent, strip_block, strip_tangent):
    row = lax.axis_index("row")
    col = lax.axis_index("col")
    at = jnp.stack(
        [row, col, row // (N_Z * N_CORE), (row // N_CORE) % N_Z, row % N_CORE]
    ).astype(jnp.int32)
    mine = pivot_block[None]
    pivot_by_y = [mine] + [along_y(mine, s) for s in range(1, N_Y)]

    def rest(s):
        at_row = lax.rem(col + s, N_Y) * 8
        return jnp.stack(
            [
                pivot_tangent,
                lax.dynamic_slice_in_dim(panel_block, at_row, 8, 0),
                lax.dynamic_slice_in_dim(panel_tangent, at_row, 8, 0),
            ]
        )

    rest_by_y = [rest(0)] + [along_y(rest(s), s) for s in range(1, N_Y)]
    pivot_pieces = gather_pieces(pivot_by_y)
    rest_pieces = gather_pieces(rest_by_y)

    def around(value, forward_first):
        left, right = along_y(value, 1), along_y(value, 3)
        far = along_y(left, 1) if forward_first else along_y(right, 3)
        return [value, left, right, far]

    parts = around(panel_block, True)
    tangent_parts = around(panel_tangent, False)

    vmem = pl.BlockSpec(memory_space=pltpu.VMEM)
    smem = pl.BlockSpec(memory_space=pltpu.SMEM)

    def matrix(*shape):
        return jax.ShapeDtypeStruct(shape, F32)

    limit = pltpu.CompilerParams(vmem_limit_bytes=56 * 2**20)
    w22, l_left, x_first = pl.pallas_call(
        first_half,
        name="first_half",
        out_shape=(matrix(HALF, HALF), matrix(PIVOT, HALF), matrix(HALF, HALF)),
        in_specs=[smem] + [vmem] * 8,
        out_specs=[vmem] * 3,
        scratch_shapes=[pltpu.VMEM((PIVOT, PIVOT), F32)],
        compiler_params=limit,
        cost_estimate=pl.CostEstimate(flops=10**9, bytes_accessed=50 * 10**6, transcendentals=0),
    )(at, *pivot_pieces)
    whole_factor, inverse = pl.pallas_call(
        second_half,
        name="second_half",
        out_shape=(matrix(PIVOT, PIVOT), matrix(PIVOT, PIVOT)),
        in_specs=[vmem] * 3,
        out_specs=[vmem] * 2,
        scratch_shapes=[pltpu.VMEM((HALF, HALF), F32)] * 3,
        compiler_params=limit,
        cost_estimate=pl.CostEstimate(flops=10**9, bytes_accessed=50 * 10**6, transcendentals=0),
    )(w22, l_left, x_first)

    local_rows, local_strip = strip_block.shape
    tile = PANEL_TILE
    narrow = pl.BlockSpec((tile, 128), lambda i: (i, 0))
    broad = pl.BlockSpec((tile, local_strip), lambda i: (i, 0))
    corner = pl.BlockSpec((8, 128), lambda i: (0, 0))
    square = pltpu.VMEM((PIVOT, PIVOT), F32)
    split_square = pltpu.VMEM((2, PIVOT, PIVOT), BF16)
    return pl.pallas_call(
        panel,
        name="panel",
        grid=(local_rows // tile,),
        out_shape=(
            matrix(8, 128),
            matrix(8, 128),
            matrix(local_rows, 128),
            matrix(local_rows, 128),
            matrix(local_rows, local_strip),
            matrix(local_rows, local_strip),
        ),
        in_specs=[smem] + [vmem] * 10 + [narrow] * 8 + [broad] * 2,
        out_specs=(corner, corner, narrow, narrow, broad, broad),
        scratch_shapes=[
            square,
            pltpu.VMEM((2, PIVOT, PIVOT), F32),
            square,
            split_square,
            split_square,
            split_square,
            split_square,
            pltpu.VMEM((2, 2 * tile, PIVOT), BF16),
            pltpu.VMEM((2, tile, PIVOT), F32),
        ],
        compiler_params=limit,
        cost_estimate=pl.CostEstimate(flops=10**10, bytes_accessed=20 * 10**6, transcendentals=0),
    )(at, whole_factor, inverse, *rest_pieces, *parts, *tangent_parts, strip_block, strip_tangent)


def solution(mesh):
    spec = P("row", "col")
    return jax.shard_map(
        body, mesh=mesh, in_specs=(spec,) * 6, out_specs=(spec,) * 6, check_vma=False
    )
```

```python
import jax
import jax.numpy as jnp
from jax import lax
from jax.experimental import pallas as pl
from jax.experimental.pallas import tpu as pltpu
from jax.sharding import PartitionSpec as P

PIVOT = 512
HALF = PIVOT // 2
BLOCK = 64
PANEL_TILE = 256
F32 = jnp.float32
BF16 = jnp.bfloat16
N_X, N_Z, N_CORE, N_Y = 4, 8, 2, 4


def exact_nt(a, b):
    return lax.dot_general(
        a, b, (((1,), (1,)), ((), ())), precision=lax.Precision.HIGHEST, preferred_element_type=F32
    )


def exact_nn(a, b):
    return lax.dot_general(
        a, b, (((1,), (0,)), ((), ())), precision=lax.Precision.HIGHEST, preferred_element_type=F32
    )


def halves(x):
    high = x.astype(BF16)
    return high, (x - high.astype(F32)).astype(BF16)


def nt(a, b):
    return lax.dot_general(a, b, (((1,), (1,)), ((), ())), preferred_element_type=F32)


def split_nt(a, b):
    return nt(a[0], b[0]) + (nt(a[0], b[1]) + nt(a[1], b[0]))


def lane(x, k):
    return jnp.broadcast_to(x[:, k : k + 1], (8, 128))


def sub(x, k):
    return jnp.broadcast_to(x[k : k + 1, :], (8, 128))


def factor_block(rows):
    rows = list(rows)
    sublane = lax.broadcasted_iota(jnp.int32, (8, 128), 0)
    done = []
    for s in range(8):
        cols = {b: [lane(rows[b], 8 * s + k) for k in range(8)] for b in range(s, 8)}
        corner = [[sub(cols[s][k], i) if i >= k else None for k in range(8)] for i in range(8)]
        scale = None
        for k in range(8):
            r = 1.0 / corner[k][k]
            m = [corner[i][k] * r if i > k else None for i in range(8)]
            for i in range(k + 1, 8):
                for j in range(k + 1, i + 1):
                    corner[i][j] = corner[i][j] - m[i] * corner[j][k]
            pivot_row = sub(rows[s], k)
            for b in range(s, 8):
                mul = cols[b][k] * r
                if b == s:
                    mul = jnp.where(sublane > k, mul, 0.0)
                for j in range(k + 1, 8):
                    cols[b][j] = cols[b][j] - mul * corner[j][k]
                rows[b] = rows[b] - mul * pivot_row
            y = lax.rsqrt(corner[k][k])
            y = y * (1.5 - 0.5 * corner[k][k] * y * y)
            scale = y if scale is None else jnp.where(sublane == k, y, scale)
        done.append(rows[s] * scale)
    return done


def merge(l_ref, x_ref, lo, h):
    a, b, c = lo, lo + h, lo + 2 * h
    t = exact_nn(l_ref[b:c, a:b], x_ref[a:b, a:b])
    x_ref[b:c, a:b] = -exact_nn(x_ref[b:c, b:c], t)


def forward(w_ref, l_ref, x_ref, lo, h):
    a, b, c = lo, lo + h, lo + 2 * h
    l21 = exact_nt(w_ref[b:c, a:b], x_ref[a:b, a:b])
    l_ref[b:c, a:b] = l21
    w_ref[b:c, b:c] = w_ref[b:c, b:c] - exact_nt(l21, l21)


def after_block(w_ref, l_ref, x_ref, j):
    h = BLOCK
    while h < HALF:
        if j % 2 == 1:
            merge(l_ref, x_ref, (j - 1) * h, h)
            j //= 2
            h *= 2
        else:
            forward(w_ref, l_ref, x_ref, j * h, h)
            return


def factor_blocks(w_ref, l_ref, x_ref, first, last):
    ri = lax.broadcasted_iota(jnp.int32, (BLOCK, BLOCK), 0)
    ci = lax.broadcasted_iota(jnp.int32, (BLOCK, BLOCK), 1)
    wide = lax.broadcasted_iota(jnp.int32, (BLOCK, 128), 1)
    eye = jnp.where(ri == ci, 1.0, 0.0).astype(F32)
    zero = jnp.zeros((BLOCK, BLOCK), F32)

    def step(j, carry):
        rows = pl.ds(pl.multiple_of(j * BLOCK, BLOCK), BLOCK)
        lanes = pl.ds(pl.multiple_of((j // 2) * 128, 128), 128)
        full = w_ref[rows, lanes]
        d = jnp.where(j % 2 == 0, full[:, :BLOCK], full[:, BLOCK:])
        both = jnp.concatenate([d, eye], axis=1)
        both = factor_block([both[8 * b : 8 * b + 8] for b in range(8)])
        both = jnp.concatenate(both, axis=0)
        low = jnp.where(ri >= ci, both[:, :BLOCK].T, 0.0)
        inverse = jnp.where(ri >= ci, both[:, BLOCK:], 0.0)
        for side in range(2):

            @pl.when(j % 2 == side)
            def _():
                put = lambda v: jnp.concatenate([v, zero] if side == 0 else [zero, v], 1)
                x_ref[rows, lanes] = put(inverse)
                l_ref[rows, lanes] = jnp.where(wide >= side * BLOCK, put(low), l_ref[rows, lanes])

        for jj in range(first, last):

            @pl.when(j == jj)
            def _():
                after_block(w_ref, l_ref, x_ref, jj)

        return carry

    lax.fori_loop(first, last, step, 0)


def col_lanes(at_ref):
    col = at_ref[1]
    return [pl.ds(pl.multiple_of(lax.rem(col + N_Y - s, N_Y) * 128, 128), 128) for s in range(N_Y)]


def spread(at_ref, pieces, at_tile, out_ref):
    x, core = at_ref[2], at_ref[3]
    lanes = col_lanes(at_ref)
    for s_core in range(N_CORE):
        for s_x in range(N_X):
            piece = pieces[s_core * N_X + s_x]
            first = lax.rem(x + N_X - s_x, N_X) * N_Z * N_CORE + lax.rem(core + s_core, N_CORE)
            for z in range(N_Z):
                rows = pl.ds(pl.multiple_of((first + z * N_CORE) * 8, 8), 8)
                for s_y in range(N_Y):
                    out_ref[rows, lanes[s_y]] = piece[(z, s_y) + at_tile]


def first_half(*refs):
    at_ref, pieces = refs[0], refs[1:9]
    w_out, l_ref, x_ref, w_ref = refs[9:]
    spread(at_ref, pieces, (), w_ref)
    l_ref[...] = jnp.zeros((PIVOT, HALF), F32)
    x_ref[...] = jnp.zeros((HALF, HALF), F32)
    factor_blocks(w_ref, l_ref, x_ref, 0, HALF // BLOCK)
    a = slice(0, HALF)
    b = slice(HALF, PIVOT)
    l21 = exact_nt(w_ref[b, a], x_ref[...])
    l_ref[b, :] = l21
    w_out[...] = w_ref[b, b] - exact_nt(l21, l21)


def second_half(w_in, l_in, x_in, l_ref, x_ref, w_ref, l22, x22):
    a = slice(0, HALF)
    b = slice(HALF, PIVOT)
    w_ref[...] = w_in[...]
    l22[...] = jnp.zeros((HALF, HALF), F32)
    x22[...] = jnp.zeros((HALF, HALF), F32)
    factor_blocks(w_ref, l22, x22, 0, HALF // BLOCK)
    l_ref[:, a] = l_in[...]
    l_ref[a, b] = jnp.zeros((HALF, HALF), F32)
    l_ref[b, b] = l22[...]
    x_ref[a, a] = x_in[...]
    x_ref[a, b] = jnp.zeros((HALF, HALF), F32)
    x_ref[b, b] = x22[...]
    x_ref[b, a] = -exact_nn(x22[...], exact_nn(l_in[b, :], x_in[...]))


def upper_nt(a, b):
    left = split_nt([v[:, :HALF] for v in a], [v[:HALF, :HALF] for v in b])
    right = split_nt(a, [v[HALF:, :] for v in b])
    return jnp.concatenate([left, right], axis=1)


def tangent_factor(x_ref, ad_ref, phi_ref):
    h = HALF
    x11, x21, x22 = x_ref[:h, :h], x_ref[h:, :h], x_ref[h:, h:]
    t11 = exact_nn(x11, ad_ref[:h, :h])
    t21 = exact_nn(x21, ad_ref[:h, :h]) + exact_nn(x22, ad_ref[h:, :h])
    t22 = exact_nn(x21, ad_ref[:h, h:]) + exact_nn(x22, ad_ref[h:, h:])
    ri = lax.broadcasted_iota(jnp.int32, (h, h), 0)
    ci = lax.broadcasted_iota(jnp.int32, (h, h), 1)
    weight = jnp.where(ri > ci, 1.0, jnp.where(ri == ci, 0.5, 0.0)).astype(F32)
    phi_ref[:h, :h] = exact_nt(t11, x11) * weight
    phi_ref[h:, :h] = exact_nt(t21, x11)
    phi_ref[h:, h:] = (exact_nt(t21, x21) + exact_nt(t22, x22)) * weight
    phi_ref[:h, h:] = jnp.zeros((h, h), F32)


def panel(*refs):
    at_ref, l_ref, x_ref = refs[:3]
    pieces = refs[3:11]
    parts, tangent_parts = refs[11:15], refs[15:19]
    strip_ref, strip_tangent_ref = refs[19:21]
    factor_out, change_out, panel_out, panel_change_out, strip_out, strip_change_out = refs[21:27]
    ad, raw, phi, xs, phis, qs, qds, rows_ref, done_ref = refs[27:]
    col = at_ref[1]
    whole = slice(None)

    @pl.when(pl.program_id(0) == 0)
    def _():
        spread(at_ref, pieces, (0,), ad)
        spread(at_ref, pieces, (1,), raw.at[0])
        spread(at_ref, pieces, (2,), raw.at[1])
        tangent_factor(x_ref, ad, phi)
        own = pl.ds(pl.multiple_of(at_ref[0] * 8, 8), 8)
        lanes = pl.ds(pl.multiple_of(col * 128, 128), 128)
        factor_out[...] = l_ref[own, lanes]
        change_out[...] = exact_nn(l_ref[own, :], phi[:, lanes])
        xs[0], xs[1] = halves(x_ref[...])
        phis[0], phis[1] = halves(phi[...])
        solved = upper_nt(halves(raw[...].reshape(2 * PIVOT, PIVOT)), [xs[0], xs[1]])
        q = halves(solved[:PIVOT])
        qs[0], qs[1] = q
        qds[0], qds[1] = halves(solved[PIVOT:] - upper_nt(q, [phis[0], phis[1]]))

    for shift, part, tangent_part in zip((0, 3, 1, 2), parts, tangent_parts):
        lanes = pl.ds(pl.multiple_of(lax.rem(col + shift, N_Y) * 128, 128), 128)
        for at, value in ((0, part[...]), (PANEL_TILE, tangent_part[...])):
            high, low = halves(value)
            rows_ref[0, at : at + PANEL_TILE, lanes] = high
            rows_ref[1, at : at + PANEL_TILE, lanes] = low
    solved = upper_nt([rows_ref[0], rows_ref[1]], [xs[0], xs[1]])
    factor = solved[:PANEL_TILE]
    factor_halves = halves(factor)
    change = solved[PANEL_TILE:] - upper_nt(factor_halves, [phis[0], phis[1]])
    change_halves = halves(change)
    done_ref[0] = factor
    done_ref[1] = change
    lanes = pl.ds(pl.multiple_of(col * 128, 128), 128)
    panel_out[...] = done_ref[0, :, lanes]
    panel_change_out[...] = done_ref[1, :, lanes]
    q = [qs[0], qs[1]]
    strip_out[...] = strip_ref[...] - split_nt(factor_halves, q)
    strip_change_out[...] = strip_tangent_ref[...] - (
        split_nt(change_halves, q) + split_nt(factor_halves, [qds[0], qds[1]])
    )


def row_index(x, z, core):
    return (x % N_X * N_Z + z % N_Z) * N_CORE + core % N_CORE


ALONG_Z = [
    [row_index(x, z, core) for z in range(N_Z)] for x in range(N_X) for core in range(N_CORE)
]

def along_y(value, s):
    return lax.ppermute(value, "col", [(c, (c + s) % N_Y) for c in range(N_Y)])


def along_x_core(value, s_x, s_core):
    pairs = [
        (row_index(x, z, core), row_index(x + s_x, z, core + s_core))
        for x in range(N_X)
        for z in range(N_Z)
        for core in range(N_CORE)
    ]
    return lax.ppermute(value, "row", pairs)


def gather_z(value):
    spread = jnp.broadcast_to(value[None], (N_Z,) + value.shape)
    return lax.all_to_all(spread, "row", 0, 0, axis_index_groups=ALONG_Z)


def body(pivot_block, pivot_tangent, panel_block, panel_tangent, strip_block, strip_tangent):
    row = lax.axis_index("row")
    col = lax.axis_index("col")
    at = jnp.stack([row, col, row // (N_Z * N_CORE), row % N_CORE]).astype(jnp.int32)

    def tiles(s):
        at_row = lax.rem(col + s, N_Y) * 8
        return jnp.stack(
            [
                pivot_block,
                pivot_tangent,
                lax.dynamic_slice_in_dim(panel_block, at_row, 8, 0),
                lax.dynamic_slice_in_dim(panel_tangent, at_row, 8, 0),
            ]
        )

    by_y = [tiles(0)] + [along_y(tiles(s), s) for s in range(1, N_Y)]
    gathered = gather_z(jnp.stack(by_y))
    pivot, rest = gathered[:, :, 0], gathered[:, :, 1:]
    pivot_pieces = [pivot] + [along_x_core(pivot, s, 0) for s in range(1, N_X)]
    pivot_pieces = pivot_pieces + [along_x_core(v, 0, 1) for v in pivot_pieces]
    own_core = [rest] + [along_x_core(rest, s, 0) for s in range(1, N_X)]
    rest_pieces = own_core + [along_x_core(v, 0, 1) for v in own_core]

    def around(value, forward_first):
        left, right = along_y(value, 1), along_y(value, 3)
        far = along_y(left, 1) if forward_first else along_y(right, 3)
        return [value, left, right, far]

    parts = around(panel_block, True)
    tangent_parts = around(panel_tangent, False)

    vmem = pl.BlockSpec(memory_space=pltpu.VMEM)
    smem = pl.BlockSpec(memory_space=pltpu.SMEM)

    def matrix(*shape):
        return jax.ShapeDtypeStruct(shape, F32)

    limit = pltpu.CompilerParams(vmem_limit_bytes=56 * 2**20)
    w22, l_left, x_first = pl.pallas_call(
        first_half,
        name="first_half",
        out_shape=(matrix(HALF, HALF), matrix(PIVOT, HALF), matrix(HALF, HALF)),
        in_specs=[smem] + [vmem] * 8,
        out_specs=[vmem] * 3,
        scratch_shapes=[pltpu.VMEM((PIVOT, PIVOT), F32)],
        compiler_params=limit,
        cost_estimate=pl.CostEstimate(flops=16 * 10**9, bytes_accessed=10**6, transcendentals=0),
    )(at, *pivot_pieces)
    whole_factor, inverse = pl.pallas_call(
        second_half,
        name="second_half",
        out_shape=(matrix(PIVOT, PIVOT), matrix(PIVOT, PIVOT)),
        in_specs=[vmem] * 3,
        out_specs=[vmem] * 2,
        scratch_shapes=[pltpu.VMEM((HALF, HALF), F32)] * 3,
        compiler_params=limit,
        cost_estimate=pl.CostEstimate(flops=16 * 10**9, bytes_accessed=10**6, transcendentals=0),
    )(w22, l_left, x_first)

    local_rows, local_strip = strip_block.shape
    tile = PANEL_TILE
    narrow = pl.BlockSpec((tile, 128), lambda i: (i, 0))
    broad = pl.BlockSpec((tile, local_strip), lambda i: (i, 0))
    corner = pl.BlockSpec((8, 128), lambda i: (0, 0))
    square = pltpu.VMEM((PIVOT, PIVOT), F32)
    split_square = pltpu.VMEM((2, PIVOT, PIVOT), BF16)
    return pl.pallas_call(
        panel,
        name="panel",
        grid=(local_rows // tile,),
        out_shape=(
            matrix(8, 128),
            matrix(8, 128),
            matrix(local_rows, 128),
            matrix(local_rows, 128),
            matrix(local_rows, local_strip),
            matrix(local_rows, local_strip),
        ),
        in_specs=[smem] + [vmem] * 10 + [narrow] * 8 + [broad] * 2,
        out_specs=(corner, corner, narrow, narrow, broad, broad),
        scratch_shapes=[
            square,
            pltpu.VMEM((2, PIVOT, PIVOT), F32),
            square,
            split_square,
            split_square,
            split_square,
            split_square,
            pltpu.VMEM((2, 2 * tile, PIVOT), BF16),
            pltpu.VMEM((2, tile, PIVOT), F32),
        ],
        compiler_params=limit,
        cost_estimate=pl.CostEstimate(flops=10**10, bytes_accessed=20 * 10**6, transcendentals=0),
    )(at, whole_factor, inverse, *rest_pieces, *parts, *tangent_parts, strip_block, strip_tangent)


def solution(mesh):
    spec = P("row", "col")
    return jax.shard_map(
        body, mesh=mesh, in_specs=(spec,) * 6, out_specs=(spec,) * 6, check_vma=False
    )
```

```python
import jax
import jax.numpy as jnp
from jax import lax
from jax.experimental import pallas as pl
from jax.experimental.pallas import tpu as pltpu
from jax.sharding import PartitionSpec as P

PIVOT = 512
HALF = PIVOT // 2
BLOCK = 128
GROUPS = BLOCK // 8
PANEL_TILE = 256
F32 = jnp.float32
BF16 = jnp.bfloat16
N_X, N_Z, N_CORE, N_Y = 4, 8, 2, 4


def thirds(x):
    first = x.astype(BF16)
    rest = x - first.astype(F32)
    second = rest.astype(BF16)
    return first, second, (rest - second.astype(F32)).astype(BF16)


def exact(a, b, a_dim, b_dim):
    a1, a2, a3 = thirds(a)
    b1, b2, b3 = thirds(b)
    left = jnp.concatenate([a1, a1, a2, a1, a2, a3], axis=a_dim)
    right = jnp.concatenate([b1, b2, b1, b3, b2, b1], axis=b_dim)
    return lax.dot_general(left, right, (((a_dim,), (b_dim,)), ((), ())), preferred_element_type=F32)


def exact_nt(a, b):
    return exact(a, b, 1, 1)


def exact_nn(a, b):
    return exact(a, b, 1, 0)


def halves(x):
    high = x.astype(BF16)
    return high, (x - high.astype(F32)).astype(BF16)


def product(a, b, contract):
    return lax.dot_general(a, b, (contract, ((), ())), preferred_element_type=F32)


def split_product(a, b, contract=((1,), (0,))):
    left = jnp.concatenate([a[0], a[0], a[1]], axis=contract[0][0])
    right = jnp.concatenate([b[0], b[1], b[0]], axis=contract[1][0])
    return product(left, right, contract)


def split_nt(a, b):
    return split_product(a, b, ((1,), (1,)))


def lane(x, k):
    return jnp.broadcast_to(x[:, k : k + 1], (8, 128))


def sub(x, k):
    return jnp.broadcast_to(x[k : k + 1, :], (8, 128))


def factor_block(rows, aside):
    rows, aside = list(rows), list(aside)
    sublane = lax.broadcasted_iota(jnp.int32, (8, 128), 0)
    half = GROUPS // 2
    for first, last in ((0, half), (half, GROUPS)):
        for s in range(first, last):
            cols = {b: [lane(rows[b], 8 * s + k) for k in range(8)] for b in range(s, last)}
            corner = [[sub(cols[s][k], i) if i >= k else None for k in range(8)] for i in range(8)]
            scale = None
            for k in range(8):
                r = 1.0 / corner[k][k]
                m = [corner[i][k] * r if i > k else None for i in range(8)]
                for i in range(k + 1, 8):
                    for j in range(k + 1, i + 1):
                        corner[i][j] = corner[i][j] - m[i] * corner[j][k]
                pivot_row = sub(rows[s], k)
                pivot_aside = sub(aside[s], k)
                for b in range(s, last):
                    mul = cols[b][k] * r
                    if b == s:
                        mul = jnp.where(sublane > k, mul, 0.0)
                    for j in range(k + 1, 8):
                        cols[b][j] = cols[b][j] - mul * corner[j][k]
                    rows[b] = rows[b] - mul * pivot_row
                    aside[b] = aside[b] - mul * pivot_aside
                y = lax.rsqrt(corner[k][k])
                y = y * (1.5 - 0.5 * corner[k][k] * y * y)
                scale = y if scale is None else jnp.where(sublane == k, y, scale)
            rows[s] = rows[s] * scale
            aside[s] = aside[s] * scale
        if first == 0:
            top = jnp.concatenate(rows[:half], axis=0)
            both = jnp.concatenate([top, jnp.concatenate(aside[:half], axis=0)], axis=1)
            change = exact(top, both, 0, 0)
            for b in range(half, GROUPS):
                rows[b] = rows[b] - change[8 * b : 8 * b + 8, :BLOCK]
                aside[b] = aside[b] - change[8 * b : 8 * b + 8, BLOCK:]
    return rows, aside


def merge(l_ref, x_ref, lo, h):
    a, b, c = lo, lo + h, lo + 2 * h
    t = exact_nn(l_ref[b:c, a:b], x_ref[a:b, a:b])
    x_ref[b:c, a:b] = -exact_nn(x_ref[b:c, b:c], t)


def forward(w_ref, l_ref, x_ref, lo, h):
    a, b, c = lo, lo + h, lo + 2 * h
    l21 = exact_nt(w_ref[b:c, a:b], x_ref[a:b, a:b])
    l_ref[b:c, a:b] = l21
    w_ref[b:c, b:c] = w_ref[b:c, b:c] - exact_nt(l21, l21)


def factor_blocks(w_ref, l_ref, x_ref):
    ri = lax.broadcasted_iota(jnp.int32, (BLOCK, BLOCK), 0)
    ci = lax.broadcasted_iota(jnp.int32, (BLOCK, BLOCK), 1)
    eye = jnp.where(ri == ci, 1.0, 0.0).astype(F32)

    def step(j, carry):
        block = pl.ds(pl.multiple_of(j * BLOCK, BLOCK), BLOCK)
        d = w_ref[block, block]
        cut = lambda v: [v[8 * b : 8 * b + 8] for b in range(GROUPS)]
        upper, inverse = factor_block(cut(d), cut(eye))
        l_ref[block, block] = jnp.where(ri >= ci, jnp.concatenate(upper, axis=0).T, 0.0)
        x_ref[block, block] = jnp.where(ri >= ci, jnp.concatenate(inverse, axis=0), 0.0)

        @pl.when(j == 0)
        def _():
            forward(w_ref, l_ref, x_ref, 0, BLOCK)

        return carry

    lax.fori_loop(0, HALF // BLOCK, step, 0)
    merge(l_ref, x_ref, 0, BLOCK)


def col_lanes(at_ref):
    col = at_ref[1]
    return [pl.ds(pl.multiple_of(lax.rem(col + N_Y - s, N_Y) * 128, 128), 128) for s in range(N_Y)]


def spread(at_ref, pieces, at_tile, out_ref):
    x, core = at_ref[2], at_ref[3]
    lanes = col_lanes(at_ref)
    for s_core in range(N_CORE):
        for s_x in range(N_X):
            piece = pieces[s_core * N_X + s_x]
            first = lax.rem(x + N_X - s_x, N_X) * N_Z * N_CORE + lax.rem(core + s_core, N_CORE)
            for z in range(N_Z):
                rows = pl.ds(pl.multiple_of((first + z * N_CORE) * 8, 8), 8)
                for s_y in range(N_Y):
                    out_ref[rows, lanes[s_y]] = piece[(z, s_y) + at_tile]


def first_half(*refs):
    at_ref, pieces = refs[0], refs[1:9]
    w_out, l_ref, x_ref, w_ref = refs[9:]
    spread(at_ref, pieces, (), w_ref)
    l_ref[...] = jnp.zeros((PIVOT, HALF), F32)
    x_ref[...] = jnp.zeros((HALF, HALF), F32)
    factor_blocks(w_ref, l_ref, x_ref)
    a = slice(0, HALF)
    b = slice(HALF, PIVOT)
    l21 = exact_nt(w_ref[b, a], x_ref[...])
    l_ref[b, :] = l21
    w_out[...] = w_ref[b, b] - exact_nt(l21, l21)


def second_half(w_in, l_in, x_in, l_ref, x_ref, w_ref, l22, x22):
    a = slice(0, HALF)
    b = slice(HALF, PIVOT)
    w_ref[...] = w_in[...]
    l22[...] = jnp.zeros((HALF, HALF), F32)
    x22[...] = jnp.zeros((HALF, HALF), F32)
    factor_blocks(w_ref, l22, x22)
    l_ref[:, a] = l_in[...]
    l_ref[a, b] = jnp.zeros((HALF, HALF), F32)
    l_ref[b, b] = l22[...]
    x_ref[a, a] = x_in[...]
    x_ref[a, b] = jnp.zeros((HALF, HALF), F32)
    x_ref[b, b] = x22[...]
    x_ref[b, a] = -exact_nn(x22[...], exact_nn(l_in[b, :], x_in[...]))


def times_upper(a, b):
    left = split_product([v[:, :HALF] for v in a], [v[:HALF, :HALF] for v in b])
    right = split_product(a, [v[:, HALF:] for v in b])
    return jnp.concatenate([left, right], axis=1)


def lower_times(a, b, contract):
    cut = (lambda v: v[:HALF]) if contract[1] == (0,) else (lambda v: v[:, :HALF])
    top = split_product([v[:HALF, :HALF] for v in a], [cut(v) for v in b], contract)
    bottom = split_product([v[HALF:] for v in a], b, contract)
    return jnp.concatenate([top, bottom], axis=0)


def tangent_factor(x_ref, ad_ref, phi_ref):
    h = HALF
    x11, x21, x22 = x_ref[:h, :h], x_ref[h:, :h], x_ref[h:, h:]
    t11 = exact_nn(x11, ad_ref[:h, :h])
    t21 = exact_nn(x21, ad_ref[:h, :h]) + exact_nn(x22, ad_ref[h:, :h])
    t22 = exact_nn(x21, ad_ref[:h, h:]) + exact_nn(x22, ad_ref[h:, h:])
    ri = lax.broadcasted_iota(jnp.int32, (h, h), 0)
    ci = lax.broadcasted_iota(jnp.int32, (h, h), 1)
    weight = jnp.where(ri > ci, 1.0, jnp.where(ri == ci, 0.5, 0.0)).astype(F32)
    phi_ref[:h, :h] = exact_nt(t11, x11) * weight
    phi_ref[h:, :h] = exact_nt(t21, x11)
    phi_ref[h:, h:] = (exact_nt(t21, x21) + exact_nt(t22, x22)) * weight
    phi_ref[:h, h:] = jnp.zeros((h, h), F32)


def panel(*refs):
    at_ref, l_ref, x_ref = refs[:3]
    pieces = refs[3:11]
    parts, tangent_parts = refs[11:15], refs[15:19]
    strip_ref, strip_tangent_ref = refs[19:21]
    factor_out, change_out, panel_out, panel_change_out, strip_out, strip_change_out = refs[21:27]
    ad, raw, phi, xs, phis, qs, qds, rows_ref, done_ref = refs[27:]
    col = at_ref[1]
    whole = slice(None)

    @pl.when(pl.program_id(0) == 0)
    def _():
        spread(at_ref, pieces, (0,), ad)
        spread(at_ref, pieces, (1,), raw.at[0])
        spread(at_ref, pieces, (2,), raw.at[1])
        tangent_factor(x_ref, ad, phi)
        own = pl.ds(pl.multiple_of(at_ref[0] * 8, 8), 8)
        lanes = pl.ds(pl.multiple_of(col * 128, 128), 128)
        factor_out[...] = l_ref[own, lanes]
        change_out[...] = exact_nn(l_ref[own, :], phi[:, lanes])
        inverse = halves(x_ref[...])
        xs[0], xs[1] = halves(x_ref[...].T)
        phis[0], phis[1] = halves(phi[...].T)
        solved = lower_times(inverse, halves(raw[...].reshape(2 * PIVOT, PIVOT)), ((1,), (1,)))
        q = halves(solved[:, :PIVOT])
        qs[0], qs[1] = q
        qds[0], qds[1] = halves(
            solved[:, PIVOT:] - lower_times(halves(phi[...]), q, ((1,), (0,)))
        )

    for shift, part, tangent_part in zip((0, 3, 1, 2), parts, tangent_parts):
        lanes = pl.ds(pl.multiple_of(lax.rem(col + shift, N_Y) * 128, 128), 128)
        for at, value in ((0, part[...]), (PANEL_TILE, tangent_part[...])):
            high, low = halves(value)
            rows_ref[0, at : at + PANEL_TILE, lanes] = high
            rows_ref[1, at : at + PANEL_TILE, lanes] = low
    solved = times_upper([rows_ref[0], rows_ref[1]], [xs[0], xs[1]])
    factor = solved[:PANEL_TILE]
    factor_halves = halves(factor)
    change = solved[PANEL_TILE:] - times_upper(factor_halves, [phis[0], phis[1]])
    change_halves = halves(change)
    done_ref[0] = factor
    done_ref[1] = change
    lanes = pl.ds(pl.multiple_of(col * 128, 128), 128)
    panel_out[...] = done_ref[0, :, lanes]
    panel_change_out[...] = done_ref[1, :, lanes]
    q = [qs[0], qs[1]]
    strip_out[...] = strip_ref[...] - split_product(factor_halves, q)
    strip_change_out[...] = strip_tangent_ref[...] - (
        split_product(change_halves, q) + split_product(factor_halves, [qds[0], qds[1]])
    )


def row_index(x, z, core):
    return (x % N_X * N_Z + z % N_Z) * N_CORE + core % N_CORE


ALONG_Z = [
    [row_index(x, z, core) for z in range(N_Z)] for x in range(N_X) for core in range(N_CORE)
]

def along_y(value, s):
    return lax.ppermute(value, "col", [(c, (c + s) % N_Y) for c in range(N_Y)])


def along_x_core(value, s_x, s_core):
    pairs = [
        (row_index(x, z, core), row_index(x + s_x, z, core + s_core))
        for x in range(N_X)
        for z in range(N_Z)
        for core in range(N_CORE)
    ]
    return lax.ppermute(value, "row", pairs)


def gather_z(value):
    spread = jnp.broadcast_to(value[None], (N_Z,) + value.shape)
    return lax.all_to_all(spread, "row", 0, 0, axis_index_groups=ALONG_Z)


def vmem_spec():
    return pl.BlockSpec(memory_space=pltpu.VMEM)


def smem_spec():
    return pl.BlockSpec(memory_space=pltpu.SMEM)


def matrix(*shape):
    return jax.ShapeDtypeStruct(shape, F32)


LIMIT = pltpu.CompilerParams(vmem_limit_bytes=56 * 2**20)


def run_panel(at, whole_factor, inverse, rest_pieces, parts, tangent_parts, strip_block, strip_tangent):
    local_rows, local_strip = strip_block.shape
    tile = PANEL_TILE
    narrow = pl.BlockSpec((tile, 128), lambda i: (i, 0))
    broad = pl.BlockSpec((tile, local_strip), lambda i: (i, 0))
    corner = pl.BlockSpec((8, 128), lambda i: (0, 0))
    square = pltpu.VMEM((PIVOT, PIVOT), F32)
    split_square = pltpu.VMEM((2, PIVOT, PIVOT), BF16)
    return pl.pallas_call(
        panel,
        name="panel",
        grid=(local_rows // tile,),
        out_shape=(
            matrix(8, 128),
            matrix(8, 128),
            matrix(local_rows, 128),
            matrix(local_rows, 128),
            matrix(local_rows, local_strip),
            matrix(local_rows, local_strip),
        ),
        in_specs=[smem_spec()] + [vmem_spec()] * 10 + [narrow] * 8 + [broad] * 2,
        out_specs=(corner, corner, narrow, narrow, broad, broad),
        scratch_shapes=[
            square,
            pltpu.VMEM((2, PIVOT, PIVOT), F32),
            square,
            split_square,
            split_square,
            split_square,
            split_square,
            pltpu.VMEM((2, 2 * tile, PIVOT), BF16),
            pltpu.VMEM((2, tile, PIVOT), F32),
        ],
        compiler_params=LIMIT,
        cost_estimate=pl.CostEstimate(flops=10**10, bytes_accessed=20 * 10**6, transcendentals=0),
    )(at, whole_factor, inverse, *rest_pieces, *parts, *tangent_parts, strip_block, strip_tangent)


def body(pivot_block, pivot_tangent, panel_block, panel_tangent, strip_block, strip_tangent):
    row = lax.axis_index("row")
    col = lax.axis_index("col")
    at = jnp.stack([row, col, row // (N_Z * N_CORE), row % N_CORE]).astype(jnp.int32)

    def tiles(s):
        at_row = lax.rem(col + s, N_Y) * 8
        return jnp.stack(
            [
                pivot_block,
                pivot_tangent,
                lax.dynamic_slice_in_dim(panel_block, at_row, 8, 0),
                lax.dynamic_slice_in_dim(panel_tangent, at_row, 8, 0),
            ]
        )

    by_y = [tiles(0)] + [along_y(tiles(s), s) for s in range(1, N_Y)]
    gathered = gather_z(jnp.stack(by_y))
    pivot, rest = gathered[:, :, 0], gathered[:, :, 1:]
    pivot_pieces = [pivot] + [along_x_core(pivot, s, 0) for s in range(1, N_X)]
    pivot_pieces = pivot_pieces + [along_x_core(v, 0, 1) for v in pivot_pieces]
    own_core = [rest] + [along_x_core(rest, s, 0) for s in range(1, N_X)]
    rest_pieces = own_core + [along_x_core(v, 0, 1) for v in own_core]

    def around(value, forward_first):
        left, right = along_y(value, 1), along_y(value, 3)
        far = along_y(left, 1) if forward_first else along_y(right, 3)
        return [value, left, right, far]

    parts = around(panel_block, True)
    tangent_parts = around(panel_tangent, False)

    w22, l_left, x_first = pl.pallas_call(
        first_half,
        name="first_half",
        out_shape=(matrix(HALF, HALF), matrix(PIVOT, HALF), matrix(HALF, HALF)),
        in_specs=[smem_spec()] + [vmem_spec()] * 8,
        out_specs=[vmem_spec()] * 3,
        scratch_shapes=[pltpu.VMEM((PIVOT, PIVOT), F32)],
        compiler_params=LIMIT,
        cost_estimate=pl.CostEstimate(flops=16 * 10**9, bytes_accessed=10**6, transcendentals=0),
    )(at, *pivot_pieces)
    whole_factor, inverse = pl.pallas_call(
        second_half,
        name="second_half",
        out_shape=(matrix(PIVOT, PIVOT), matrix(PIVOT, PIVOT)),
        in_specs=[vmem_spec()] * 3,
        out_specs=[vmem_spec()] * 2,
        scratch_shapes=[pltpu.VMEM((HALF, HALF), F32)] * 3,
        compiler_params=LIMIT,
        cost_estimate=pl.CostEstimate(flops=16 * 10**9, bytes_accessed=10**6, transcendentals=0),
    )(w22, l_left, x_first)

    return run_panel(
        at, whole_factor, inverse, rest_pieces, parts, tangent_parts, strip_block, strip_tangent
    )


def solution(mesh):
    spec = P("row", "col")
    return jax.shard_map(
        body, mesh=mesh, in_specs=(spec,) * 6, out_specs=(spec,) * 6, check_vma=False
    )
```

```python
import jax
import jax.numpy as jnp
from jax import lax
from jax.experimental import pallas as pl
from jax.experimental.pallas import tpu as pltpu
from jax.sharding import PartitionSpec as P

PIVOT = 512
HALF = PIVOT // 2
BLOCK = 128
GROUPS = BLOCK // 8
PANEL_TILE = 256
F32 = jnp.float32
BF16 = jnp.bfloat16
N_X, N_Z, N_CORE, N_Y = 4, 8, 2, 4


def thirds(x):
    first = x.astype(BF16)
    rest = x - first.astype(F32)
    second = rest.astype(BF16)
    return first, second, (rest - second.astype(F32)).astype(BF16)


def exact(a, b, a_dim, b_dim):
    a1, a2, a3 = thirds(a)
    b1, b2, b3 = thirds(b)
    left = jnp.concatenate([a1, a1, a2, a1, a2, a3], axis=a_dim)
    right = jnp.concatenate([b1, b2, b1, b3, b2, b1], axis=b_dim)
    return lax.dot_general(left, right, (((a_dim,), (b_dim,)), ((), ())), preferred_element_type=F32)


def exact_nt(a, b):
    return exact(a, b, 1, 1)


def exact_nn(a, b):
    return exact(a, b, 1, 0)


def halves(x):
    high = x.astype(BF16)
    return high, (x - high.astype(F32)).astype(BF16)


def product(a, b, contract):
    return lax.dot_general(a, b, (contract, ((), ())), preferred_element_type=F32)


def split_product(a, b, contract=((1,), (0,))):
    left = jnp.concatenate([a[0], a[0], a[1]], axis=contract[0][0])
    right = jnp.concatenate([b[0], b[1], b[0]], axis=contract[1][0])
    return product(left, right, contract)


def split_nt(a, b):
    return split_product(a, b, ((1,), (1,)))


def lane(x, k):
    return jnp.broadcast_to(x[:, k : k + 1], (8, 128))


def sub(x, k):
    return jnp.broadcast_to(x[k : k + 1, :], (8, 128))


def factor_block(rows, aside):
    rows, aside = list(rows), list(aside)
    sublane = lax.broadcasted_iota(jnp.int32, (8, 128), 0)
    half = GROUPS // 2
    for first, last in ((0, half), (half, GROUPS)):
        for s in range(first, last):
            cols = {b: [lane(rows[b], 8 * s + k) for k in range(8)] for b in range(s, last)}
            corner = [[sub(cols[s][k], i) if i >= k else None for k in range(8)] for i in range(8)]
            scale = None
            for k in range(8):
                r = 1.0 / corner[k][k]
                m = [corner[i][k] * r if i > k else None for i in range(8)]
                for i in range(k + 1, 8):
                    for j in range(k + 1, i + 1):
                        corner[i][j] = corner[i][j] - m[i] * corner[j][k]
                pivot_row = sub(rows[s], k)
                pivot_aside = sub(aside[s], k)
                for b in range(s, last):
                    mul = cols[b][k] * r
                    if b == s:
                        mul = jnp.where(sublane > k, mul, 0.0)
                    for j in range(k + 1, 8):
                        cols[b][j] = cols[b][j] - mul * corner[j][k]
                    rows[b] = rows[b] - mul * pivot_row
                    aside[b] = aside[b] - mul * pivot_aside
                y = lax.rsqrt(corner[k][k])
                y = y * (1.5 - 0.5 * corner[k][k] * y * y)
                scale = y if scale is None else jnp.where(sublane == k, y, scale)
            rows[s] = rows[s] * scale
            aside[s] = aside[s] * scale
        if first == 0:
            top = jnp.concatenate(rows[:half], axis=0)
            both = jnp.concatenate([top, jnp.concatenate(aside[:half], axis=0)], axis=1)
            change = exact(top, both, 0, 0)
            for b in range(half, GROUPS):
                rows[b] = rows[b] - change[8 * b : 8 * b + 8, :BLOCK]
                aside[b] = aside[b] - change[8 * b : 8 * b + 8, BLOCK:]
    return rows, aside


def merge(l_ref, x_ref, lo, h):
    a, b, c = lo, lo + h, lo + 2 * h
    t = exact_nn(l_ref[b:c, a:b], x_ref[a:b, a:b])
    x_ref[b:c, a:b] = -exact_nn(x_ref[b:c, b:c], t)


def forward(w_ref, l_ref, x_ref, lo, h):
    a, b, c = lo, lo + h, lo + 2 * h
    l21 = exact_nt(w_ref[b:c, a:b], x_ref[a:b, a:b])
    l_ref[b:c, a:b] = l21
    w_ref[b:c, b:c] = w_ref[b:c, b:c] - exact_nt(l21, l21)


def factor_one(w_ref, l_ref, x_ref, block):
    ri = lax.broadcasted_iota(jnp.int32, (BLOCK, BLOCK), 0)
    ci = lax.broadcasted_iota(jnp.int32, (BLOCK, BLOCK), 1)
    eye = jnp.where(ri == ci, 1.0, 0.0).astype(F32)
    cut = lambda v: [v[8 * b : 8 * b + 8] for b in range(GROUPS)]
    upper, inverse = factor_block(cut(w_ref[block, block]), cut(eye))
    l_ref[block, block] = jnp.where(ri >= ci, jnp.concatenate(upper, axis=0).T, 0.0)
    x_ref[block, block] = jnp.where(ri >= ci, jnp.concatenate(inverse, axis=0), 0.0)


def factor_two(w_ref, l_ref, x_ref):
    def step(j, carry):
        factor_one(w_ref, l_ref, x_ref, pl.ds(pl.multiple_of(j * BLOCK, BLOCK), BLOCK))

        @pl.when(j == 0)
        def _():
            forward(w_ref, l_ref, x_ref, 0, BLOCK)

        return carry

    lax.fori_loop(0, HALF // BLOCK, step, 0)
    merge(l_ref, x_ref, 0, BLOCK)


def col_lanes(at_ref):
    col = at_ref[1]
    return [pl.ds(pl.multiple_of(lax.rem(col + N_Y - s, N_Y) * 128, 128), 128) for s in range(N_Y)]


def spread(at_ref, pieces, at_tile, out_ref):
    x, core = at_ref[2], at_ref[3]
    lanes = col_lanes(at_ref)
    for s_core in range(N_CORE):
        for s_x in range(N_X):
            piece = pieces[s_core * N_X + s_x]
            first = lax.rem(x + N_X - s_x, N_X) * N_Z * N_CORE + lax.rem(core + s_core, N_CORE)
            for z in range(N_Z):
                rows = pl.ds(pl.multiple_of((first + z * N_CORE) * 8, 8), 8)
                for s_y in range(N_Y):
                    out_ref[rows, lanes[s_y]] = piece[(z, s_y) + at_tile]


def first_blocks(*refs):
    at_ref, pieces = refs[0], refs[1:9]
    w22, l_ref, x_ref, l22, x22, w_ref = refs[10:]
    spread(at_ref, pieces, (), w_ref)
    l_ref[...] = jnp.zeros((PIVOT, HALF), F32)
    x_ref[...] = jnp.zeros((HALF, HALF), F32)
    l22[...] = jnp.zeros((HALF, HALF), F32)
    x22[...] = jnp.zeros((HALF, HALF), F32)
    factor_two(w_ref, l_ref, x_ref)
    a = slice(0, HALF)
    b = slice(HALF, PIVOT)
    l21 = exact_nt(w_ref[b, a], x_ref[...])
    l_ref[b, :] = l21
    w22[...] = w_ref[b, b] - exact_nt(l21, l21)
    factor_one(w22, l22, x22, slice(0, BLOCK))
    forward(w22, l22, x22, 0, BLOCK)


def last_block(w22, l_in, x_in, l22_in, x22_in, l_ref, x_ref, l22, x22):
    a = slice(0, HALF)
    b = slice(HALF, PIVOT)
    l22[...] = l22_in[...]
    x22[...] = x22_in[...]
    factor_one(w22, l22, x22, slice(BLOCK, HALF))
    merge(l22, x22, 0, BLOCK)
    l_ref[:, a] = l_in[...]
    l_ref[a, b] = jnp.zeros((HALF, HALF), F32)
    l_ref[b, b] = l22[...]
    x_ref[a, a] = x_in[...]
    x_ref[a, b] = jnp.zeros((HALF, HALF), F32)
    x_ref[b, b] = x22[...]
    x_ref[b, a] = -exact_nn(x22[...], exact_nn(l_in[b, :], x_in[...]))


def times_upper(a, b):
    left = split_product([v[:, :HALF] for v in a], [v[:HALF, :HALF] for v in b])
    right = split_product(a, [v[:, HALF:] for v in b])
    return jnp.concatenate([left, right], axis=1)


def lower_times(a, b, contract):
    cut = (lambda v: v[:HALF]) if contract[1] == (0,) else (lambda v: v[:, :HALF])
    top = split_product([v[:HALF, :HALF] for v in a], [cut(v) for v in b], contract)
    bottom = split_product([v[HALF:] for v in a], b, contract)
    return jnp.concatenate([top, bottom], axis=0)


def tangent_factor(x_ref, ad_ref, phi_ref):
    h = HALF
    x11, x21, x22 = x_ref[:h, :h], x_ref[h:, :h], x_ref[h:, h:]
    t11 = exact_nn(x11, ad_ref[:h, :h])
    t21 = exact_nn(x21, ad_ref[:h, :h]) + exact_nn(x22, ad_ref[h:, :h])
    t22 = exact_nn(x21, ad_ref[:h, h:]) + exact_nn(x22, ad_ref[h:, h:])
    ri = lax.broadcasted_iota(jnp.int32, (h, h), 0)
    ci = lax.broadcasted_iota(jnp.int32, (h, h), 1)
    weight = jnp.where(ri > ci, 1.0, jnp.where(ri == ci, 0.5, 0.0)).astype(F32)
    phi_ref[:h, :h] = exact_nt(t11, x11) * weight
    phi_ref[h:, :h] = exact_nt(t21, x11)
    phi_ref[h:, h:] = (exact_nt(t21, x21) + exact_nt(t22, x22)) * weight
    phi_ref[:h, h:] = jnp.zeros((h, h), F32)


def panel(*refs):
    at_ref, l_ref, x_ref = refs[:3]
    pieces = refs[3:11]
    parts, tangent_parts = refs[11:15], refs[15:19]
    strip_ref, strip_tangent_ref = refs[19:21]
    factor_out, change_out, panel_out, panel_change_out, strip_out, strip_change_out = refs[21:27]
    ad, raw, phi, xs, phis, qs, qds, rows_ref, done_ref = refs[27:]
    col = at_ref[1]
    whole = slice(None)

    @pl.when(pl.program_id(0) == 0)
    def _():
        spread(at_ref, pieces, (0,), ad)
        spread(at_ref, pieces, (1,), raw.at[0])
        spread(at_ref, pieces, (2,), raw.at[1])
        tangent_factor(x_ref, ad, phi)
        own = pl.ds(pl.multiple_of(at_ref[0] * 8, 8), 8)
        lanes = pl.ds(pl.multiple_of(col * 128, 128), 128)
        factor_out[...] = l_ref[own, lanes]
        change_out[...] = exact_nn(l_ref[own, :], phi[:, lanes])
        inverse = halves(x_ref[...])
        xs[0], xs[1] = halves(x_ref[...].T)
        phis[0], phis[1] = halves(phi[...].T)
        solved = lower_times(inverse, halves(raw[...].reshape(2 * PIVOT, PIVOT)), ((1,), (1,)))
        q = halves(solved[:, :PIVOT])
        qs[0], qs[1] = q
        qds[0], qds[1] = halves(
            solved[:, PIVOT:] - lower_times(halves(phi[...]), q, ((1,), (0,)))
        )

    for shift, part, tangent_part in zip((0, 3, 1, 2), parts, tangent_parts):
        lanes = pl.ds(pl.multiple_of(lax.rem(col + shift, N_Y) * 128, 128), 128)
        for at, value in ((0, part[...]), (PANEL_TILE, tangent_part[...])):
            high, low = halves(value)
            rows_ref[0, at : at + PANEL_TILE, lanes] = high
            rows_ref[1, at : at + PANEL_TILE, lanes] = low
    solved = times_upper([rows_ref[0], rows_ref[1]], [xs[0], xs[1]])
    factor = solved[:PANEL_TILE]
    factor_halves = halves(factor)
    change = solved[PANEL_TILE:] - times_upper(factor_halves, [phis[0], phis[1]])
    change_halves = halves(change)
    done_ref[0] = factor
    done_ref[1] = change
    lanes = pl.ds(pl.multiple_of(col * 128, 128), 128)
    panel_out[...] = done_ref[0, :, lanes]
    panel_change_out[...] = done_ref[1, :, lanes]
    q = [qs[0], qs[1]]
    strip_out[...] = strip_ref[...] - split_product(factor_halves, q)
    strip_change_out[...] = strip_tangent_ref[...] - (
        split_product(change_halves, q) + split_product(factor_halves, [qds[0], qds[1]])
    )


def row_index(x, z, core):
    return (x % N_X * N_Z + z % N_Z) * N_CORE + core % N_CORE


ALONG_Z = [
    [row_index(x, z, core) for z in range(N_Z)] for x in range(N_X) for core in range(N_CORE)
]

def along_y(value, s):
    return lax.ppermute(value, "col", [(c, (c + s) % N_Y) for c in range(N_Y)])


def along_x_core(value, s_x, s_core):
    pairs = [
        (row_index(x, z, core), row_index(x + s_x, z, core + s_core))
        for x in range(N_X)
        for z in range(N_Z)
        for core in range(N_CORE)
    ]
    return lax.ppermute(value, "row", pairs)


def gather_z(value):
    spread = jnp.broadcast_to(value[None], (N_Z,) + value.shape)
    return lax.all_to_all(spread, "row", 0, 0, axis_index_groups=ALONG_Z)


def vmem_spec():
    return pl.BlockSpec(memory_space=pltpu.VMEM)


def smem_spec():
    return pl.BlockSpec(memory_space=pltpu.SMEM)


def matrix(*shape):
    return jax.ShapeDtypeStruct(shape, F32)


LIMIT = pltpu.CompilerParams(vmem_limit_bytes=56 * 2**20)


def run_panel(at, whole_factor, inverse, rest_pieces, parts, tangent_parts, strip_block, strip_tangent):
    local_rows, local_strip = strip_block.shape
    tile = PANEL_TILE
    narrow = pl.BlockSpec((tile, 128), lambda i: (i, 0))
    broad = pl.BlockSpec((tile, local_strip), lambda i: (i, 0))
    corner = pl.BlockSpec((8, 128), lambda i: (0, 0))
    stacked = lambda which: pl.BlockSpec((None, tile, 128), lambda i: (which, i, 0))
    square = pltpu.VMEM((PIVOT, PIVOT), F32)
    split_square = pltpu.VMEM((2, PIVOT, PIVOT), BF16)
    return pl.pallas_call(
        panel,
        name="panel",
        grid=(local_rows // tile,),
        out_shape=(
            matrix(8, 128),
            matrix(8, 128),
            matrix(local_rows, 128),
            matrix(local_rows, 128),
            matrix(local_rows, local_strip),
            matrix(local_rows, local_strip),
        ),
        in_specs=[smem_spec()] + [vmem_spec()] * 10 + [narrow, *[stacked(0)] * 3]
        + [narrow, *[stacked(1)] * 3]
        + [broad] * 2,
        out_specs=(corner, corner, narrow, narrow, broad, broad),
        scratch_shapes=[
            square,
            pltpu.VMEM((2, PIVOT, PIVOT), F32),
            square,
            split_square,
            split_square,
            split_square,
            split_square,
            pltpu.VMEM((2, 2 * tile, PIVOT), BF16),
            pltpu.VMEM((2, tile, PIVOT), F32),
        ],
        compiler_params=LIMIT,
        cost_estimate=pl.CostEstimate(flops=10**10, bytes_accessed=20 * 10**6, transcendentals=0),
    )(at, whole_factor, inverse, *rest_pieces, *parts, *tangent_parts, strip_block, strip_tangent)


def body(pivot_block, pivot_tangent, panel_block, panel_tangent, strip_block, strip_tangent):
    row = lax.axis_index("row")
    col = lax.axis_index("col")
    at = jnp.stack([row, col, row // (N_Z * N_CORE), row % N_CORE]).astype(jnp.int32)

    def tiles(s):
        at_row = lax.rem(col + s, N_Y) * 8
        return jnp.stack(
            [
                pivot_block,
                pivot_tangent,
                lax.dynamic_slice_in_dim(panel_block, at_row, 8, 0),
                lax.dynamic_slice_in_dim(panel_tangent, at_row, 8, 0),
            ]
        )

    by_y = [tiles(0)] + [along_y(tiles(s), s) for s in range(1, N_Y)]
    gathered = gather_z(jnp.stack(by_y))
    pivot, rest = gathered[:, :, 0], gathered[:, :, 1:]
    pivot_pieces = [pivot] + [along_x_core(pivot, s, 0) for s in range(1, N_X)]
    pivot_pieces = pivot_pieces + [along_x_core(v, 0, 1) for v in pivot_pieces]
    own_core = [rest] + [along_x_core(rest, s, 0) for s in range(1, N_X)]
    rest_pieces = own_core + [along_x_core(v, 0, 1) for v in own_core]

    both = jnp.stack([panel_block, panel_tangent])
    left, right = along_y(both, 1), along_y(both, 3)
    far = along_y(left, 1)
    parts = [panel_block, left, right, far]
    tangent_parts = [panel_tangent, left, right, far]

    quarter = matrix(HALF, HALF)
    factored = pl.pallas_call(
        first_blocks,
        name="first_blocks",
        out_shape=(quarter, matrix(PIVOT, HALF), quarter, quarter, quarter),
        in_specs=[smem_spec()] + [vmem_spec()] * 8 + [pl.BlockSpec(memory_space=pl.ANY)],
        out_specs=[vmem_spec()] * 5,
        scratch_shapes=[pltpu.VMEM((PIVOT, PIVOT), F32)],
        compiler_params=LIMIT,
        cost_estimate=pl.CostEstimate(flops=22 * 10**9, bytes_accessed=10**6, transcendentals=0),
    )(at, *pivot_pieces, right)
    whole_factor, inverse = pl.pallas_call(
        last_block,
        name="last_block",
        out_shape=(matrix(PIVOT, PIVOT), matrix(PIVOT, PIVOT)),
        in_specs=[vmem_spec()] * 5,
        out_specs=[vmem_spec()] * 2,
        scratch_shapes=[pltpu.VMEM((HALF, HALF), F32)] * 2,
        compiler_params=LIMIT,
        cost_estimate=pl.CostEstimate(flops=10 * 10**9, bytes_accessed=10**6, transcendentals=0),
    )(*factored)

    return run_panel(
        at, whole_factor, inverse, rest_pieces, parts, tangent_parts, strip_block, strip_tangent
    )


def solution(mesh):
    spec = P("row", "col")
    return jax.shard_map(
        body, mesh=mesh, in_specs=(spec,) * 6, out_specs=(spec,) * 6, check_vma=False
    )
```

```python
import jax
import jax.numpy as jnp
from jax import lax
from jax.experimental import pallas as pl
from jax.experimental.pallas import tpu as pltpu
from jax.sharding import PartitionSpec as P

PIVOT = 512
HALF = PIVOT // 2
BLOCK = 128
GROUPS = BLOCK // 8
PANEL_TILE = 256
F32 = jnp.float32
BF16 = jnp.bfloat16
N_X, N_Z, N_CORE, N_Y = 4, 8, 2, 4


def thirds(x):
    first = x.astype(BF16)
    rest = x - first.astype(F32)
    second = rest.astype(BF16)
    return first, second, (rest - second.astype(F32)).astype(BF16)


def exact(a, b, a_dim, b_dim):
    a1, a2, a3 = thirds(a)
    b1, b2, b3 = thirds(b)
    left = jnp.concatenate([a1, a1, a2, a1, a2, a3], axis=a_dim)
    right = jnp.concatenate([b1, b2, b1, b3, b2, b1], axis=b_dim)
    return lax.dot_general(left, right, (((a_dim,), (b_dim,)), ((), ())), preferred_element_type=F32)


def exact_nt(a, b):
    return exact(a, b, 1, 1)


def exact_nn(a, b):
    return exact(a, b, 1, 0)


def halves(x):
    high = x.astype(BF16)
    return high, (x - high.astype(F32)).astype(BF16)


def product(a, b, contract):
    return lax.dot_general(a, b, (contract, ((), ())), preferred_element_type=F32)


def split_product(a, b, contract=((1,), (0,))):
    left = jnp.concatenate([a[0], a[0], a[1]], axis=contract[0][0])
    right = jnp.concatenate([b[0], b[1], b[0]], axis=contract[1][0])
    return product(left, right, contract)


def end_to_end(a):
    return jnp.concatenate([a[0], a[0], a[1]], axis=1)


def store_stacked(ref, b):
    depth = b[0].shape[0]
    for i, half in enumerate((b[0], b[1], b[0])):
        ref[i * depth : (i + 1) * depth] = half


def split_nt(a, b):
    return split_product(a, b, ((1,), (1,)))


def lane(x, k):
    return jnp.broadcast_to(x[:, k : k + 1], (8, 128))


def sub(x, k):
    return jnp.broadcast_to(x[k : k + 1, :], (8, 128))


def factor_block(rows, aside):
    rows, aside = list(rows), list(aside)
    sublane = lax.broadcasted_iota(jnp.int32, (8, 128), 0)
    half = GROUPS // 2
    for first, last in ((0, half), (half, GROUPS)):
        for s in range(first, last):
            cols = {b: [lane(rows[b], 8 * s + k) for k in range(8)] for b in range(s, last)}
            corner = [[sub(cols[s][k], i) if i >= k else None for k in range(8)] for i in range(8)]
            scale = None
            for k in range(8):
                r = 1.0 / corner[k][k]
                m = [corner[i][k] * r if i > k else None for i in range(8)]
                for i in range(k + 1, 8):
                    for j in range(k + 1, i + 1):
                        corner[i][j] = corner[i][j] - m[i] * corner[j][k]
                pivot_row = sub(rows[s], k)
                pivot_aside = sub(aside[s], k)
                for b in range(s, last):
                    mul = cols[b][k] * r
                    if b == s:
                        mul = jnp.where(sublane > k, mul, 0.0)
                    for j in range(k + 1, 8):
                        cols[b][j] = cols[b][j] - mul * corner[j][k]
                    rows[b] = rows[b] - mul * pivot_row
                    aside[b] = aside[b] - mul * pivot_aside
                y = lax.rsqrt(corner[k][k])
                y = y * (1.5 - 0.5 * corner[k][k] * y * y)
                scale = y if scale is None else jnp.where(sublane == k, y, scale)
            rows[s] = rows[s] * scale
            aside[s] = aside[s] * scale
        if first == 0:
            top = jnp.concatenate(rows[:half], axis=0)
            both = jnp.concatenate([top, jnp.concatenate(aside[:half], axis=0)], axis=1)
            change = exact(top, both, 0, 0)
            for b in range(half, GROUPS):
                rows[b] = rows[b] - change[8 * b : 8 * b + 8, :BLOCK]
                aside[b] = aside[b] - change[8 * b : 8 * b + 8, BLOCK:]
    return rows, aside


def merge(l_ref, x_ref, lo, h):
    a, b, c = lo, lo + h, lo + 2 * h
    t = exact_nn(l_ref[b:c, a:b], x_ref[a:b, a:b])
    x_ref[b:c, a:b] = -exact_nn(x_ref[b:c, b:c], t)


def forward(w_ref, l_ref, x_ref, lo, h):
    a, b, c = lo, lo + h, lo + 2 * h
    l21 = exact_nt(w_ref[b:c, a:b], x_ref[a:b, a:b])
    l_ref[b:c, a:b] = l21
    w_ref[b:c, b:c] = w_ref[b:c, b:c] - exact_nt(l21, l21)


def factor_one(w_ref, l_ref, x_ref, block):
    ri = lax.broadcasted_iota(jnp.int32, (BLOCK, BLOCK), 0)
    ci = lax.broadcasted_iota(jnp.int32, (BLOCK, BLOCK), 1)
    eye = jnp.where(ri == ci, 1.0, 0.0).astype(F32)
    cut = lambda v: [v[8 * b : 8 * b + 8] for b in range(GROUPS)]
    upper, inverse = factor_block(cut(w_ref[block, block]), cut(eye))
    l_ref[block, block] = jnp.where(ri >= ci, jnp.concatenate(upper, axis=0).T, 0.0)
    x_ref[block, block] = jnp.where(ri >= ci, jnp.concatenate(inverse, axis=0), 0.0)


def factor_two(w_ref, l_ref, x_ref):
    def step(j, carry):
        factor_one(w_ref, l_ref, x_ref, pl.ds(pl.multiple_of(j * BLOCK, BLOCK), BLOCK))

        @pl.when(j == 0)
        def _():
            forward(w_ref, l_ref, x_ref, 0, BLOCK)

        return carry

    lax.fori_loop(0, HALF // BLOCK, step, 0)
    merge(l_ref, x_ref, 0, BLOCK)


def col_lanes(at_ref):
    col = at_ref[1]
    return [pl.ds(pl.multiple_of(lax.rem(col + N_Y - s, N_Y) * 128, 128), 128) for s in range(N_Y)]


def spread(at_ref, pieces, at_tile, out_ref):
    x, core = at_ref[2], at_ref[3]
    lanes = col_lanes(at_ref)
    for s_core in range(N_CORE):
        for s_x in range(N_X):
            piece = pieces[s_core * N_X + s_x]
            first = lax.rem(x + N_X - s_x, N_X) * N_Z * N_CORE + lax.rem(core + s_core, N_CORE)
            for z in range(N_Z):
                rows = pl.ds(pl.multiple_of((first + z * N_CORE) * 8, 8), 8)
                for s_y in range(N_Y):
                    out_ref[rows, lanes[s_y]] = piece[(z, s_y) + at_tile]


def first_blocks(*refs):
    at_ref, pieces = refs[0], refs[1:9]
    x_ref, t_ref, own_left, w_last, l_low, x_mid = refs[10:16]
    w_ref, l_ref, w22, l22, x22 = refs[16:]
    spread(at_ref, pieces, (), w_ref)
    l_ref[...] = jnp.zeros((PIVOT, HALF), F32)
    x_ref[...] = jnp.zeros((HALF, HALF), F32)
    factor_two(w_ref, l_ref, x_ref)
    a = slice(0, HALF)
    b = slice(HALF, PIVOT)
    l21 = exact_nt(w_ref[b, a], x_ref[...])
    l_ref[b, :] = l21
    w22[...] = w_ref[b, b] - exact_nt(l21, l21)
    factor_one(w22, l22, x22, slice(0, BLOCK))
    forward(w22, l22, x22, 0, BLOCK)
    t_ref[...] = exact_nn(l_ref[b, :], x_ref[...])
    own_left[...] = l_ref[pl.ds(pl.multiple_of(at_ref[0] * 8, 8), 8), :]
    w_last[...] = w22[BLOCK:, BLOCK:]
    l_low[...] = l22[:, :BLOCK]
    x_mid[...] = x22[:BLOCK, :BLOCK]


def last_block(at_ref, t_in, own_left, w_last, l_low, x_mid, own_ref, x_low, w22, l22, x22):
    zero = jnp.zeros((BLOCK, BLOCK), F32)
    w22[BLOCK:, BLOCK:] = w_last[...]
    l22[:, :BLOCK] = l_low[...]
    l22[:BLOCK, BLOCK:] = zero
    x22[:BLOCK, :BLOCK] = x_mid[...]
    x22[:BLOCK, BLOCK:] = zero
    factor_one(w22, l22, x22, slice(BLOCK, HALF))
    merge(l22, x22, 0, BLOCK)
    x_low[:, HALF:] = x22[...]
    x_low[:, :HALF] = -exact_nn(x22[...], t_in[...])
    row = at_ref[0] * 8 - HALF
    right = l22[pl.ds(pl.multiple_of(jnp.maximum(row, 0), 8), 8), :]
    own_ref[:, :HALF] = own_left[...]
    own_ref[:, HALF:] = jnp.where(row >= 0, right, 0.0)


def store_upper(left_ref, right_ref, b):
    store_stacked(left_ref, [v[:HALF, :HALF] for v in b])
    store_stacked(right_ref, [v[:, HALF:] for v in b])


def times_upper(a, left_ref, right_ref):
    left = product(end_to_end([v[:, :HALF] for v in a]), left_ref[...], ((1,), (0,)))
    right = product(end_to_end(a), right_ref[...], ((1,), (0,)))
    return jnp.concatenate([left, right], axis=1)


def lower_times(a, b, contract):
    cut = (lambda v: v[:HALF]) if contract[1] == (0,) else (lambda v: v[:, :HALF])
    top = split_product([v[:HALF, :HALF] for v in a], [cut(v) for v in b], contract)
    bottom = split_product([v[HALF:] for v in a], b, contract)
    return jnp.concatenate([top, bottom], axis=0)


def tangent_factor(x_ref, ad_ref, phi_ref):
    h = HALF
    x11, x21, x22 = x_ref[:h, :h], x_ref[h:, :h], x_ref[h:, h:]
    t11 = exact_nn(x11, ad_ref[:h, :h])
    t21 = exact_nn(x21, ad_ref[:h, :h]) + exact_nn(x22, ad_ref[h:, :h])
    t22 = exact_nn(x21, ad_ref[:h, h:]) + exact_nn(x22, ad_ref[h:, h:])
    ri = lax.broadcasted_iota(jnp.int32, (h, h), 0)
    ci = lax.broadcasted_iota(jnp.int32, (h, h), 1)
    weight = jnp.where(ri > ci, 1.0, jnp.where(ri == ci, 0.5, 0.0)).astype(F32)
    phi_ref[:h, :h] = exact_nt(t11, x11) * weight
    phi_ref[h:, :h] = exact_nt(t21, x11)
    phi_ref[h:, h:] = (exact_nt(t21, x21) + exact_nt(t22, x22)) * weight
    phi_ref[:h, h:] = jnp.zeros((h, h), F32)


def panel(*refs):
    at_ref, l_ref, x_first, x_low = refs[:4]
    pieces = refs[4:12]
    parts, tangent_parts = refs[12:16], refs[16:20]
    strip_ref, strip_tangent_ref = refs[20:22]
    factor_out, change_out, panel_out, panel_change_out, strip_out, strip_change_out = refs[22:28]
    ad, raw, phi, xs_l, xs_r, phis_l, phis_r, qs, rows_ref, done_ref, x_ref = refs[28:]
    col = at_ref[1]
    whole = slice(None)

    @pl.when(pl.program_id(0) == 0)
    def _():
        spread(at_ref, pieces, (0,), ad)
        spread(at_ref, pieces, (1,), raw.at[0])
        spread(at_ref, pieces, (2,), raw.at[1])
        x_ref[:HALF, :HALF] = x_first[...]
        x_ref[:HALF, HALF:] = jnp.zeros((HALF, HALF), F32)
        x_ref[HALF:, :] = x_low[...]
        tangent_factor(x_ref, ad, phi)
        lanes = pl.ds(pl.multiple_of(col * 128, 128), 128)
        factor_out[...] = l_ref[:, lanes]
        change_out[...] = exact_nn(l_ref[...], phi[:, lanes])
        inverse = halves(x_ref[...])
        store_upper(xs_l, xs_r, halves(x_ref[...].T))
        store_upper(phis_l, phis_r, halves(phi[...].T))
        solved = lower_times(inverse, halves(raw[...].reshape(2 * PIVOT, PIVOT)), ((1,), (1,)))
        q = halves(solved[:, :PIVOT])
        store_stacked(qs.at[: 3 * PIVOT], q)
        store_stacked(
            qs.at[3 * PIVOT :],
            halves(solved[:, PIVOT:] - lower_times(halves(phi[...]), q, ((1,), (0,)))),
        )

    for shift, part, tangent_part in zip((0, 3, 1, 2), parts, tangent_parts):
        lanes = pl.ds(pl.multiple_of(lax.rem(col + shift, N_Y) * 128, 128), 128)
        for at, value in ((0, part[...]), (PANEL_TILE, tangent_part[...])):
            high, low = halves(value)
            rows_ref[0, at : at + PANEL_TILE, lanes] = high
            rows_ref[1, at : at + PANEL_TILE, lanes] = low
    solved = times_upper([rows_ref[0], rows_ref[1]], xs_l, xs_r)
    factor = solved[:PANEL_TILE]
    factor_halves = halves(factor)
    change = solved[PANEL_TILE:] - times_upper(factor_halves, phis_l, phis_r)
    done_ref[0] = factor
    done_ref[1] = change
    lanes = pl.ds(pl.multiple_of(col * 128, 128), 128)
    panel_out[...] = done_ref[0, :, lanes]
    panel_change_out[...] = done_ref[1, :, lanes]
    by_factor = end_to_end(factor_halves)
    strip_out[...] = strip_ref[...] - product(by_factor, qs[: 3 * PIVOT], ((1,), (0,)))
    by_both = jnp.concatenate([end_to_end(halves(change)), by_factor], axis=1)
    strip_change_out[...] = strip_tangent_ref[...] - product(by_both, qs[...], ((1,), (0,)))


def row_index(x, z, core):
    return (x % N_X * N_Z + z % N_Z) * N_CORE + core % N_CORE


ALONG_Z = [
    [row_index(x, z, core) for z in range(N_Z)] for x in range(N_X) for core in range(N_CORE)
]

def along_y(value, s):
    return lax.ppermute(value, "col", [(c, (c + s) % N_Y) for c in range(N_Y)])


def along_x_core(value, s_x, s_core):
    pairs = [
        (row_index(x, z, core), row_index(x + s_x, z, core + s_core))
        for x in range(N_X)
        for z in range(N_Z)
        for core in range(N_CORE)
    ]
    return lax.ppermute(value, "row", pairs)


def gather_z(value):
    spread = jnp.broadcast_to(value[None], (N_Z,) + value.shape)
    return lax.all_to_all(spread, "row", 0, 0, axis_index_groups=ALONG_Z)


def vmem_spec():
    return pl.BlockSpec(memory_space=pltpu.VMEM)


def smem_spec():
    return pl.BlockSpec(memory_space=pltpu.SMEM)


def matrix(*shape):
    return jax.ShapeDtypeStruct(shape, F32)


LIMIT = pltpu.CompilerParams(vmem_limit_bytes=56 * 2**20)


def run_panel(at, own_factor, inverse, rest_pieces, parts, tangent_parts, strip_block, strip_tangent):
    local_rows, local_strip = strip_block.shape
    tile = PANEL_TILE
    narrow = pl.BlockSpec((tile, 128), lambda i: (i, 0))
    broad = pl.BlockSpec((tile, local_strip), lambda i: (i, 0))
    corner = pl.BlockSpec((8, 128), lambda i: (0, 0))
    stacked = lambda which: pl.BlockSpec((None, tile, 128), lambda i: (which, i, 0))
    square = pltpu.VMEM((PIVOT, PIVOT), F32)
    return pl.pallas_call(
        panel,
        name="panel",
        grid=(local_rows // tile,),
        out_shape=(
            matrix(8, 128),
            matrix(8, 128),
            matrix(local_rows, 128),
            matrix(local_rows, 128),
            matrix(local_rows, local_strip),
            matrix(local_rows, local_strip),
        ),
        in_specs=[smem_spec()] + [vmem_spec()] * 11 + [narrow, *[stacked(0)] * 3]
        + [narrow, *[stacked(1)] * 3]
        + [broad] * 2,
        out_specs=(corner, corner, narrow, narrow, broad, broad),
        scratch_shapes=[
            square,
            pltpu.VMEM((2, PIVOT, PIVOT), F32),
            square,
            pltpu.VMEM((3 * HALF, HALF), BF16),
            pltpu.VMEM((3 * PIVOT, HALF), BF16),
            pltpu.VMEM((3 * HALF, HALF), BF16),
            pltpu.VMEM((3 * PIVOT, HALF), BF16),
            pltpu.VMEM((6 * PIVOT, PIVOT), BF16),
            pltpu.VMEM((2, 2 * tile, PIVOT), BF16),
            pltpu.VMEM((2, tile, PIVOT), F32),
            square,
        ],
        compiler_params=LIMIT,
        cost_estimate=pl.CostEstimate(flops=10**10, bytes_accessed=20 * 10**6, transcendentals=0),
    )(at, own_factor, *inverse, *rest_pieces, *parts, *tangent_parts, strip_block, strip_tangent)


def body(pivot_block, pivot_tangent, panel_block, panel_tangent, strip_block, strip_tangent):
    row = lax.axis_index("row")
    col = lax.axis_index("col")
    at = jnp.stack([row, col, row // (N_Z * N_CORE), row % N_CORE]).astype(jnp.int32)

    def tiles(s):
        at_row = lax.rem(col + s, N_Y) * 8
        return jnp.stack(
            [
                pivot_block,
                pivot_tangent,
                lax.dynamic_slice_in_dim(panel_block, at_row, 8, 0),
                lax.dynamic_slice_in_dim(panel_tangent, at_row, 8, 0),
            ]
        )

    by_y = [tiles(0)] + [along_y(tiles(s), s) for s in range(1, N_Y)]
    gathered = gather_z(jnp.stack(by_y))
    pivot, rest = gathered[:, :, 0], gathered[:, :, 1:]
    pivot_pieces = [pivot] + [along_x_core(pivot, s, 0) for s in range(1, N_X)]
    pivot_pieces = pivot_pieces + [along_x_core(v, 0, 1) for v in pivot_pieces]
    own_core = [rest] + [along_x_core(rest, s, 0) for s in range(1, N_X)]
    rest_pieces = own_core + [along_x_core(v, 0, 1) for v in own_core]

    both = jnp.stack([panel_block, panel_tangent])
    left, right = along_y(both, 1), along_y(both, 3)
    far = along_y(left, 1)
    parts = [panel_block, left, right, far]
    tangent_parts = [panel_tangent, left, right, far]

    quarter = matrix(HALF, HALF)
    small = matrix(BLOCK, BLOCK)
    x_first, *factored = pl.pallas_call(
        first_blocks,
        name="first_blocks",
        out_shape=(quarter, quarter, matrix(8, HALF), small, matrix(HALF, BLOCK), small),
        in_specs=[smem_spec()] + [vmem_spec()] * 8 + [pl.BlockSpec(memory_space=pl.ANY)],
        out_specs=[vmem_spec()] * 6,
        scratch_shapes=[pltpu.VMEM((PIVOT, PIVOT), F32), pltpu.VMEM((PIVOT, HALF), F32)]
        + [pltpu.VMEM((HALF, HALF), F32)] * 3,
        compiler_params=LIMIT,
        cost_estimate=pl.CostEstimate(flops=22 * 10**9, bytes_accessed=10**6, transcendentals=0),
    )(at, *pivot_pieces, right)
    own_factor, x_low = pl.pallas_call(
        last_block,
        name="last_block",
        out_shape=(matrix(8, PIVOT), matrix(HALF, PIVOT)),
        in_specs=[smem_spec()] + [vmem_spec()] * 5,
        out_specs=[vmem_spec()] * 2,
        scratch_shapes=[pltpu.VMEM((HALF, HALF), F32)] * 3,
        compiler_params=LIMIT,
        cost_estimate=pl.CostEstimate(flops=10 * 10**9, bytes_accessed=10**6, transcendentals=0),
    )(at, *factored)
    inverse = (x_first, x_low)

    return run_panel(
        at, own_factor, inverse, rest_pieces, parts, tangent_parts, strip_block, strip_tangent
    )


def solution(mesh):
    spec = P("row", "col")
    return jax.shard_map(
        body, mesh=mesh, in_specs=(spec,) * 6, out_specs=(spec,) * 6, check_vma=False
    )
```
